32 devices in a mesh: grp: 2 (over y), lat: 4 (over z), chan: 2 (over x), pair: 2 (over core).
Axes of the slice: x: 2, y: 2, z: 4, core: 2. Of those that a mesh axis runs over, the one named last changes fastest.
Arguments:
- grid_field: bfloat16 [4, 352, 256, 1440], P(('grp', 'pair'), 'lat', 'chan'), parts along dimension 0, may hold values from -6 to 6
- legendre: bfloat16 [2, 32, 12, 352, 192], P('pair', None, None, 'lat'), may hold values from -0.3125 to 0.3125
- owned_blocks: int32 [32], replicated, may hold values from 0 to 31, as said below
Outputs:
- spectrum: bfloat16 [32, 4, 12, 192, 512], P('lat', ('grp', 'pair'), None, None, 'chan'), parts along dimension 1
The draws below stay inside these ranges and needn't reach their ends.
There are 2 independent parts, one for each index of `grp`. The reference program is written for one: setup_inputs(seed, part) draws one part's arguments, and reference() takes and returns one part's arrays. A program takes and returns all parts, laid end to end along the dimension named above; an argument that names none is the same for every part. Nothing has to cross between parts.
Inputs may be any that keep to these rules, and one draw needn't show every extreme that they name: `owned_blocks`: every block number appears exactly once; slots 2q and 2q + 1 hold two blocks whose numbers add up to 31.
All inputs are finite; a program needn't handle non-finite values.
Results may differ from the reference program's by a relative error of at most 0.009.
Values may be sent and summed in bfloat16 or wider, within the bound.
A program may use at most 320 MiB of HBM per device.

```python
import math
import jax
import jax.numpy as jnp
from jax import lax

NH = 352
NLON = 1440
CH = 256
L = 384
NB = 32
MB = 12
KMAX = 192
LB = 88


def draw_owned_blocks(key, part):
    half_count = NB // 2
    lower = jax.random.permutation(jax.random.fold_in(key, 11), half_count).astype(jnp.int32)
    flipped = jax.random.randint(jax.random.fold_in(key, 12), (half_count,), 0, 2).astype(jnp.int32)
    upper = (NB - 1 - lower).astype(jnp.int32)
    leading = jnp.where(flipped == 1, upper, lower)
    trailing = jnp.where(flipped == 1, lower, upper)
    return jnp.stack([leading, trailing], axis=1).reshape(NB).astype(jnp.int32)


def shard_levels(key, shape, shards, low, top_value):
    def one(position, parts):
        heights = jax.random.uniform(jax.random.fold_in(jax.random.fold_in(key, 6), position), (parts,), jnp.float32, low / len(shards), top_value / len(shards))
        return jnp.repeat(jnp.exp(heights), shape[position] // parts).reshape((-1,) + (1,) * (len(shape) - position - 1))

    loudness = one(*shards[0])
    for cut in shards[1:]:
        loudness = loudness * one(*cut)
    return loudness


def noise(own_key, dims, scale, reach, split=(), held_as=jnp.bfloat16):
    loudness = shard_levels(own_key, dims, split, -0.22, 0.18) if split else 1.0
    drawn = jax.random.normal(own_key, dims, jnp.float32) * scale * loudness
    return jnp.minimum(jnp.maximum(drawn, -reach), reach).astype(held_as)


def setup_inputs(seed: int = 0, part: int = 0) -> dict:
    key_list = jax.random.split(jax.random.key(seed), 4)
    part_keys = jax.random.split(jax.random.fold_in(key_list[3], part), 4)
    return {
        "grid_field": noise(part_keys[0], (2, NH, CH, NLON), 1.0, 6.0, ((0, 2), (1, 4), (2, 2))),
        "legendre": noise(key_list[1], (2, NB, MB, NH, KMAX), NH ** -0.5, 0.3125, ((0, 2), (3, 4))),
        "owned_blocks": draw_owned_blocks(jax.random.fold_in(key_list[3], 71), part),
    }


def fourier_table(order_count, lon_count):
    orders = jnp.arange(order_count, dtype=jnp.int32)
    points = jnp.arange(lon_count, dtype=jnp.int32)
    phase_index = orders[:, None] * points[None, :] % lon_count
    angles = phase_index.astype(jnp.float32) * (2.0 * math.pi / lon_count)
    scaling = 1.0 / math.sqrt(lon_count)
    return (jnp.stack([jnp.cos(angles), -jnp.sin(angles)], axis=1) * scaling).astype(jnp.bfloat16)

def reference(grid_field, legendre, owned_blocks):
    wave_table = fourier_table(L, NLON).astype(jnp.float32)

    def transform_half(hemisphere):
        return jnp.einsum('mrn,tcn->mtcr', wave_table, hemisphere.astype(jnp.float32)).astype(jnp.bfloat16)
    fourier = lax.map(transform_half, grid_field)
    northern = fourier[0].astype(jnp.float32)
    southern = fourier[1].astype(jnp.float32)
    folded = jnp.stack([northern + southern, northern - southern]).astype(jnp.bfloat16)
    folded = folded.reshape(2 * NB, MB, NH, 2 * CH)
    weights = legendre.reshape(2 * NB, MB, NH, KMAX)
    band_total = NH // LB

    def block_sum(pieces):
        table_block, values = pieces
        table_band = table_block.astype(jnp.float32).reshape(MB, band_total, LB, KMAX)
        value_band = values.astype(jnp.float32).reshape(MB, band_total, LB, 2 * CH)
        partial_sums = jnp.einsum('jgtk,jgtx->gjkx', table_band, value_band).astype(jnp.bfloat16)
        partial_sums = lax.optimization_barrier(partial_sums)
        return lax.optimization_barrier(jnp.sum(partial_sums.astype(jnp.float32), axis=0))
    summed = lax.map(block_sum, (weights, folded)).reshape(2, NB, MB, KMAX, 2 * CH)
    blocks = jnp.arange(NB, dtype=jnp.int32)
    limits = KMAX - MB // 2 * blocks
    row_index = jnp.arange(KMAX, dtype=jnp.int32)
    inside = row_index[None, :] < limits[:, None]
    summed = jnp.where(inside[None, :, None, :, None], summed, jnp.zeros_like(summed))
    chosen = jnp.take(summed, owned_blocks.astype(jnp.int32), axis=1)
    return jnp.transpose(chosen, (1, 0, 2, 3, 4)).astype(jnp.bfloat16)
```

```python
import functools
import math

import jax
import jax.numpy as jnp
from jax import lax
from jax.experimental import pallas as pl
from jax.experimental.pallas import tpu as pltpu
from jax.sharding import PartitionSpec as P


def swapped(value, axis, distance):
    mask = 2**distance
    pairs = [(source, source ^ mask) for source in range(lax.axis_size(axis))]
    return lax.ppermute(value, axis, pairs)


def trig(index, lon_count):
    angles = (index % lon_count).astype(jnp.float32) * (2.0 * math.pi / lon_count)
    return jnp.cos(angles), jnp.sin(angles)


def wave_rows(base, step):
    cos_a, sin_a = (v[..., None, :] for v in base)
    cos_b, sin_b = step
    cos_sum = cos_a * cos_b - sin_a * sin_b
    sin_sum = sin_a * cos_b + cos_a * sin_b
    return jnp.stack([cos_sum, -sin_sum], axis=-2).astype(jnp.bfloat16)


def pack_kernel(kmax, half, blocks, total, meta, lo_ref, hi_ref, own_ref, mir_ref, out_ref):
    pair = pl.program_id(0)
    lo = meta[pair]
    sign = meta[pl.num_programs(0)].astype(jnp.float32)
    limit = kmax - half * lo
    width = out_ref.shape[3]
    place = lax.broadcasted_iota(jnp.int32, (width, kmax), 0)
    row = lax.broadcasted_iota(jnp.int32, (width, kmax), 1)
    pick_lo = ((place == row) & (place < limit)).astype(jnp.float32).astype(jnp.bfloat16)
    pick_hi = ((place == row + limit) & (place < total)).astype(jnp.float32).astype(jnp.bfloat16)
    nt = (((1,), (1,)), ((), ()))
    for j in range(lo_ref.shape[1]):
        tables = [
            lax.dot_general(pick, ref[0, j], nt, preferred_element_type=jnp.float32).astype(jnp.bfloat16)
            for pick, ref in ((pick_lo, lo_ref), (pick_hi, hi_ref))
        ]
        for r in range(out_ref.shape[2]):
            acc = None
            for side in range(2):
                own = own_ref[0, side, j, r].astype(jnp.float32)
                mir = mir_ref[0, side, j, r].astype(jnp.float32)
                folded = (mir + sign * own).astype(jnp.bfloat16)
                term = jnp.dot(tables[side], folded, preferred_element_type=jnp.float32)
                acc = term if acc is None else acc + term
            out_ref[0, j, r] = acc.astype(jnp.bfloat16)


def pack(tables, own, mirrored, lows, sign, orders_step):
    nb, mb, band, kmax = tables.shape
    pairs, _, _, parts, _, chan = own.shape
    half = mb // 2
    total = 2 * kmax - half * (nb - 1)
    width = -(-total // 8) * 8
    meta = jnp.concatenate([lows, sign[None]])
    value_spec = pl.BlockSpec(
        (1, 2, orders_step, parts, band, chan), lambda p, j, m: (p, 0, j, 0, 0, 0)
    )
    return pl.pallas_call(
        functools.partial(pack_kernel, kmax, half, nb, total),
        out_shape=jax.ShapeDtypeStruct((pairs, mb, parts, width, chan), jnp.bfloat16),
        grid_spec=pltpu.PrefetchScalarGridSpec(
            num_scalar_prefetch=1,
            grid=(pairs, mb // orders_step),
            in_specs=[
                pl.BlockSpec((1, orders_step, band, kmax), lambda p, j, m: (m[p], j, 0, 0)),
                pl.BlockSpec((1, orders_step, band, kmax), lambda p, j, m: (nb - 1 - m[p], j, 0, 0)),
                value_spec,
                value_spec,
            ],
            out_specs=pl.BlockSpec(
                (1, orders_step, parts, width, chan), lambda p, j, m: (p, j, 0, 0, 0)
            ),
        ),
        cost_estimate=pl.CostEstimate(
            flops=4 * own.size * width,
            bytes_accessed=4 * own.size + 4 * pairs * mb * band * kmax + 2 * pairs * mb * parts * width * chan,
            transcendentals=0,
        ),
        name="pack",
    )(meta, tables, tables, own, mirrored)


def unpack_kernel(nb, half, total, meta, sum_ref, *rest):
    out_ref = rest[-1]
    block = meta[pl.program_id(0)]
    kmax, columns = out_ref.shape[3:]
    width, chan = sum_ref.shape[2:]
    low = jnp.minimum(block, nb - 1 - block)
    shift = jnp.where(2 * block < nb, 0, kmax - half * low)
    limit = kmax - half * block
    row = lax.broadcasted_iota(jnp.int32, (kmax, width), 0)
    place = lax.broadcasted_iota(jnp.int32, (kmax, width), 1)
    pick = ((place == row + shift) & (row < limit)).astype(jnp.float32).astype(jnp.bfloat16)
    source = lax.broadcasted_iota(jnp.int32, (chan, columns), 0)
    target = lax.broadcasted_iota(jnp.int32, (chan, columns), 1)
    parts = sum_ref.shape[1]
    spread = [
        (target == parts * source + r).astype(jnp.float32).astype(jnp.bfloat16) for r in range(parts)
    ]
    for j in range(sum_ref.shape[0]):
        acc = None
        for r in range(parts):
            rows = jnp.dot(pick, sum_ref[j, r], preferred_element_type=jnp.float32).astype(jnp.bfloat16)
            term = jnp.dot(rows, spread[r], preferred_element_type=jnp.float32)
            acc = term if acc is None else acc + term
        out_ref[0, 0, j] = acc.astype(jnp.bfloat16)


def unpack(summed, blocks, previous, first, slots, kmax, nb, orders_step):
    mb, parts, width, chan = summed.shape
    half = mb // 2
    total = 2 * kmax - half * (nb - 1)
    operands = [blocks, summed]
    in_specs = [pl.BlockSpec((orders_step, parts, width, chan), lambda s, j, m: (j, 0, 0, 0))]
    aliases = {}
    if previous is not None:
        operands.append(previous)
        in_specs.append(pl.BlockSpec(memory_space=pl.ANY))
        aliases = {2: 0}
    return pl.pallas_call(
        functools.partial(unpack_kernel, nb, half, total),
        out_shape=jax.ShapeDtypeStruct((slots, 1, mb, kmax, parts * chan), jnp.bfloat16),
        grid_spec=pltpu.PrefetchScalarGridSpec(
            num_scalar_prefetch=1,
            grid=(2, mb // orders_step),
            in_specs=in_specs,
            out_specs=pl.BlockSpec(
                (1, 1, orders_step, kmax, parts * chan), lambda s, j, m: (first + s, 0, j, 0, 0)
            ),
        ),
        input_output_aliases=aliases,
        cost_estimate=pl.CostEstimate(
            flops=4 * mb * parts * kmax * width * chan,
            bytes_accessed=4 * summed.size + 4 * mb * kmax * parts * chan,
            transcendentals=0,
        ),
        name="unpack",
    )(*operands)


def per_device(grid_field, legendre, owned_blocks):
    lat_count = lax.axis_size("lat")
    tables = legendre[0]
    nb, mb, band, kmax = tables.shape
    field = grid_field[0]
    _, chan, lon = field.shape
    slots = nb // lat_count
    rounds = slots // 2
    orders_step = 3 if mb % 3 == 0 else 1
    sign = 1 - 2 * lax.axis_index("pair").astype(jnp.int32)
    by_pair = owned_blocks.reshape(lat_count, rounds, 2)
    lows = jnp.min(by_pair, axis=2)
    both = jnp.stack([lows, nb - 1 - lows], axis=2)
    points = jnp.arange(lon, dtype=jnp.int32)
    base = trig(both[..., None] * mb % lon * points, lon)
    step = trig(jnp.arange(mb, dtype=jnp.int32)[:, None] * points, lon)
    scale = 1.0 / math.sqrt(lon)
    step = tuple(v * scale for v in step)
    mine = lax.dynamic_slice_in_dim(owned_blocks, lax.axis_index("lat") * slots, slots)
    result = None
    for i in range(rounds):
        waves = wave_rows(tuple(v[:, i] for v in base), step)
        own = jnp.einsum(
            "pbjrn,tcn->pbjrtc", waves, field, preferred_element_type=jnp.float32
        ).astype(jnp.bfloat16)
        mirrored = swapped(own, "pair", 0)
        packed = pack(tables, own, mirrored, lows[:, i], sign, orders_step)
        summed = lax.psum_scatter(packed, "lat", scatter_dimension=0, tiled=True)
        result = unpack(
            summed[0], lax.slice_in_dim(mine, 2 * i, 2 * i + 2), result, 2 * i, slots, kmax, nb, orders_step
        )
    return result


def solution(mesh):
    return jax.shard_map(
        per_device,
        mesh=mesh,
        in_specs=(P(("grp", "pair"), "lat", "chan", None), P("pair", None, None, "lat", None), P()),
        out_specs=P("lat", ("grp", "pair"), None, None, "chan"),
        check_vma=False,
    )
```

```python
import functools
import math

import jax
import jax.numpy as jnp
from jax import lax
from jax.experimental import pallas as pl
from jax.experimental.pallas import tpu as pltpu
from jax.sharding import PartitionSpec as P


def swapped(value, axis, distance):
    mask = 2**distance
    pairs = [(source, source ^ mask) for source in range(lax.axis_size(axis))]
    return lax.ppermute(value, axis, pairs)


def trig(index, lon_count):
    angles = (index % lon_count).astype(jnp.float32) * (2.0 * math.pi / lon_count)
    return jnp.cos(angles), jnp.sin(angles)


def wave_rows(base, step):
    cos_a, sin_a = (v[..., None, :] for v in base)
    cos_b, sin_b = step
    cos_sum = cos_a * cos_b - sin_a * sin_b
    sin_sum = sin_a * cos_b + cos_a * sin_b
    return jnp.stack([cos_sum, -sin_sum], axis=-2).astype(jnp.bfloat16)


def pack_kernel(kmax, half, blocks, total, meta, lo_ref, hi_ref, own_ref, mir_ref, out_ref):
    pair = pl.program_id(0)
    lo = meta[pair]
    sign = meta[pl.num_programs(0)].astype(jnp.float32)
    limit = kmax - half * lo
    width = out_ref.shape[3]
    place = lax.broadcasted_iota(jnp.int32, (width, kmax), 0)
    row = lax.broadcasted_iota(jnp.int32, (width, kmax), 1)
    pick_lo = ((place == row) & (place < limit)).astype(jnp.float32).astype(jnp.bfloat16)
    pick_hi = ((place == row + limit) & (place < total)).astype(jnp.float32).astype(jnp.bfloat16)
    nt = (((1,), (1,)), ((), ()))

    def order(j, carry):
        tables = [
            lax.dot_general(pick, ref[0, j], nt, preferred_element_type=jnp.float32).astype(jnp.bfloat16)
            for pick, ref in ((pick_lo, lo_ref), (pick_hi, hi_ref))
        ]
        parts, chan = out_ref.shape[2], out_ref.shape[4]
        folded = [[], []]
        for side in range(2):
            for r in range(parts):
                own = own_ref[0, side, j, r].astype(jnp.float32)
                mir = mir_ref[0, side, j, r].astype(jnp.float32)
                folded[side].append((mir + sign * own).astype(jnp.bfloat16))
        if chan % 128 == 0:
            wide = [jnp.concatenate(values, axis=1) for values in folded]
            acc = jnp.dot(tables[0], wide[0], preferred_element_type=jnp.float32) + jnp.dot(
                tables[1], wide[1], preferred_element_type=jnp.float32
            )
            for r in range(parts):
                out_ref[0, j, r] = acc[:, r * chan : (r + 1) * chan].astype(jnp.bfloat16)
        else:
            for r in range(parts):
                acc = jnp.dot(tables[0], folded[0][r], preferred_element_type=jnp.float32) + jnp.dot(
                    tables[1], folded[1][r], preferred_element_type=jnp.float32
                )
                out_ref[0, j, r] = acc.astype(jnp.bfloat16)
        return carry

    lax.fori_loop(0, lo_ref.shape[1], order, 0)


def pack(tables, own, mirrored, lows, sign, start, orders_step):
    nb, mb, band, kmax = tables.shape
    pairs, _, count, parts, _, chan = own.shape
    half = mb // 2
    first = start // orders_step
    total = 2 * kmax - half * (nb - 1)
    width = -(-total // 8) * 8
    meta = jnp.concatenate([lows, sign[None]])
    value_spec = pl.BlockSpec(
        (1, 2, orders_step, parts, band, chan), lambda p, j, m: (p, 0, j, 0, 0, 0)
    )
    return pl.pallas_call(
        functools.partial(pack_kernel, kmax, half, nb, total),
        out_shape=jax.ShapeDtypeStruct((pairs, count, parts, width, chan), jnp.bfloat16),
        grid_spec=pltpu.PrefetchScalarGridSpec(
            num_scalar_prefetch=1,
            grid=(pairs, count // orders_step),
            in_specs=[
                pl.BlockSpec((1, orders_step, band, kmax), lambda p, j, m: (m[p], first + j, 0, 0)),
                pl.BlockSpec((1, orders_step, band, kmax), lambda p, j, m: (nb - 1 - m[p], first + j, 0, 0)),
                value_spec,
                value_spec,
            ],
            out_specs=pl.BlockSpec(
                (1, orders_step, parts, width, chan), lambda p, j, m: (p, j, 0, 0, 0)
            ),
        ),
        cost_estimate=pl.CostEstimate(
            flops=4 * own.size * width,
            bytes_accessed=4 * own.size + 4 * pairs * count * band * kmax + 2 * pairs * count * parts * width * chan,
            transcendentals=0,
        ),
        name="pack",
    )(meta, tables, tables, own, mirrored)


def unpack_kernel(nb, half, total, meta, sum_ref, *rest):
    out_ref = rest[-1]
    block = meta[pl.program_id(0)]
    kmax, columns = out_ref.shape[3:]
    width, chan = sum_ref.shape[3:]
    low = jnp.minimum(block, nb - 1 - block)
    shift = jnp.where(2 * block < nb, 0, kmax - half * low)
    limit = kmax - half * block
    row = lax.broadcasted_iota(jnp.int32, (kmax, width), 0)
    place = lax.broadcasted_iota(jnp.int32, (kmax, width), 1)
    pick = ((place == row + shift) & (row < limit)).astype(jnp.float32).astype(jnp.bfloat16)
    parts = sum_ref.shape[2]
    group = parts if chan % 128 == 0 else 1
    source = lax.broadcasted_iota(jnp.int32, (group * chan, columns), 0)
    target = lax.broadcasted_iota(jnp.int32, (group * chan, columns), 1)
    spread = [
        (target == parts * (source % chan) + source // chan + r).astype(jnp.float32).astype(jnp.bfloat16)
        for r in range(0, parts, group)
    ]

    def order(j, carry):
        acc = None
        for n, r in enumerate(range(0, parts, group)):
            values = [sum_ref[0, j, r + k] for k in range(group)]
            values = jnp.concatenate(values, axis=1) if group > 1 else values[0]
            rows = jnp.dot(pick, values, preferred_element_type=jnp.float32).astype(jnp.bfloat16)
            term = jnp.dot(rows, spread[n], preferred_element_type=jnp.float32)
            acc = term if acc is None else acc + term
        out_ref[0, 0, j] = acc.astype(jnp.bfloat16)
        return carry

    lax.fori_loop(0, sum_ref.shape[1], order, 0)


def unpack(summed, blocks, previous, start, kmax, nb, mb, orders_step):
    rounds, count, parts, width, chan = summed.shape
    slots = 2 * rounds
    begin = start // orders_step
    half = mb // 2
    total = 2 * kmax - half * (nb - 1)
    operands = [blocks, summed]
    in_specs = [pl.BlockSpec((1, orders_step, parts, width, chan), lambda s, j, m: (s // 2, j, 0, 0, 0))]
    aliases = {}
    if previous is not None:
        operands.append(previous)
        in_specs.append(pl.BlockSpec(memory_space=pl.ANY))
        aliases = {2: 0}
    return pl.pallas_call(
        functools.partial(unpack_kernel, nb, half, total),
        out_shape=jax.ShapeDtypeStruct((slots, 1, mb, kmax, parts * chan), jnp.bfloat16),
        grid_spec=pltpu.PrefetchScalarGridSpec(
            num_scalar_prefetch=1,
            grid=(slots, count // orders_step),
            in_specs=in_specs,
            out_specs=pl.BlockSpec(
                (1, 1, orders_step, kmax, parts * chan), lambda s, j, m: (s, 0, begin + j, 0, 0)
            ),
        ),
        input_output_aliases=aliases,
        cost_estimate=pl.CostEstimate(
            flops=4 * slots * count * parts * kmax * width * chan,
            bytes_accessed=4 * summed.size + 4 * slots * count * kmax * parts * chan,
            transcendentals=0,
        ),
        name="unpack",
    )(*operands)


def chunks(mb):
    cuts = sorted({0, mb // 12, mb // 4, mb * 7 // 12, mb})
    return [(a, b - a) for a, b in zip(cuts, cuts[1:])]


def per_device(grid_field, legendre, owned_blocks):
    lat_count = lax.axis_size("lat")
    tables = legendre[0]
    nb, mb, band, kmax = tables.shape
    field = grid_field[0]
    _, chan, lon = field.shape
    slots = nb // lat_count
    rounds = slots // 2
    orders_step = 3 if mb % 3 == 0 else 1
    sign = 1 - 2 * lax.axis_index("pair").astype(jnp.int32)
    lows = jnp.min(owned_blocks.reshape(nb // 2, 2), axis=1)
    both = jnp.stack([lows, nb - 1 - lows], axis=1)
    points = jnp.arange(lon, dtype=jnp.int32)
    base = trig(both.reshape(nb)[:, None] * mb % lon * points, lon)
    step = trig(jnp.arange(mb, dtype=jnp.int32)[:, None] * points, lon)
    scale = 1.0 / math.sqrt(lon)
    step = tuple(v * scale for v in step)
    mine = lax.dynamic_slice_in_dim(owned_blocks, lax.axis_index("lat") * slots, slots)
    result = None
    for start, count in chunks(mb):
        waves = wave_rows(
            tuple(v.reshape(nb // 2, 2, lon) for v in base),
            tuple(v[start : start + count] for v in step),
        )
        own = jnp.einsum(
            "pbjrn,tcn->pbjrtc", waves, field, preferred_element_type=jnp.float32
        ).astype(jnp.bfloat16)
        mirrored = swapped(own, "pair", 0)
        orders_step = max(k for k in (4, 3, 2, 1) if start % k == 0 and count % k == 0)
        packed = pack(tables, own, mirrored, lows, sign, start, orders_step)
        summed = lax.psum_scatter(packed, "lat", scatter_dimension=0, tiled=True)
        result = unpack(summed, mine, result, start, kmax, nb, mb, orders_step)
    return result


def solution(mesh):
    return jax.shard_map(
        per_device,
        mesh=mesh,
        in_specs=(P(("grp", "pair"), "lat", "chan", None), P("pair", None, None, "lat", None), P()),
        out_specs=P("lat", ("grp", "pair"), None, None, "chan"),
        check_vma=False,
    )
```
